32 devices in a mesh: grp: 4 (over z), seq: 8 (over y, x, core).
Axes of the slice: x: 2, y: 2, z: 4, core: 2. Of those that a mesh axis runs over, the one named last changes fastest.
Arguments:
- fine_rows: bfloat16 [4, 1024, 2048], P('grp', 'seq'), may hold values from -6 to 6
- segment_ids: int32 [4, 1024], P('grp', 'seq'), may hold values from 0 to 7, as said below
- pool_gain: float32 [2048], replicated, may hold values from 0.1 to 1.9
- w_in: bfloat16 [2048, 8192], P('grp', 'seq'), may hold values from -0.125 to 0.125
- w_gate: bfloat16 [8192, 16384], P('grp', 'seq'), may hold values from -0.0625 to 0.0625
- w_up: bfloat16 [8192, 16384], P('grp', 'seq'), may hold values from -0.0625 to 0.0625
- w_down: bfloat16 [16384, 8192], P('seq', 'grp'), may hold values from -0.046875 to 0.046875
- out_grad: bfloat16 [4, 64, 8192], P('grp'), may hold values from -6 to 6
Outputs:
- coarse_out: bfloat16 [4, 64, 8192], P('grp', None, 'seq')
- fine_grad: bfloat16 [4, 1024, 2048], P('grp', 'seq')
The draws below stay inside these ranges and needn't reach their ends.
Inputs may be any that keep to these rules, and one draw needn't show every extreme that they name: `segment_ids`: within each shard of 128 consecutive bytes the numbers count the shard's segments from 0 upward, never falling, every segment one byte or more; a shard holds 4 to 8 segments, some shard of every document exactly 8, and every document 48 segments in all.
All inputs are finite; a program needn't handle non-finite values.
Results may differ from the reference program's by a relative error of at most 0.02.
Values may be sent and summed in bfloat16 or wider, within the bound.
A program may use at most 192 MiB of HBM per device.

```python
import jax
import jax.numpy as jnp
from jax import lax

DF = 2048
D = 8192
FF = 16384
TOK_DEV = 128
SEG_CAP = 8
DOCS = 4
DOC_LEN = 1024
ROWS = 64
N_SEQ = 8


def draw_segment_ids(key, part):
    shards = DOC_LEN // TOK_DEV
    pair_count = shards // 2
    key_load, key_order, key_cut = jax.random.split(key, 3)
    first_loads = jax.random.randint(key_load, (DOCS, pair_count), SEG_CAP // 2, SEG_CAP + 1)
    first_loads = first_loads.at[:, 0].set(SEG_CAP)
    shard_loads = jnp.concatenate([first_loads, 3 * SEG_CAP // 2 - first_loads], axis=1)
    order_keys = jax.random.split(key_order, DOCS)
    orders = jax.vmap(lambda subkey: jax.random.permutation(subkey, shards))(order_keys)
    shard_loads = jnp.take_along_axis(shard_loads, orders, axis=1)
    cut_keys = jax.random.split(key_cut, DOCS * shards)
    cut_ranks = jax.vmap(lambda subkey: jax.random.permutation(subkey, TOK_DEV - 1))(cut_keys)
    cut_ranks = cut_ranks.reshape(DOCS, shards, TOK_DEV - 1)
    cut_marks = (cut_ranks < shard_loads[:, :, None] - 1).astype(jnp.int32)
    leading = jnp.zeros((DOCS, shards, 1), jnp.int32)
    segment_index = jnp.concatenate([leading, jnp.cumsum(cut_marks, axis=2)], axis=2)
    return segment_index.reshape(DOCS, DOC_LEN).astype(jnp.int32)


def block_levels(own_key, shape, cuts, smallest, largest):
    gain = 1.0
    for axis_at, parts in cuts:
        draws = jax.random.uniform(jax.random.fold_in(jax.random.fold_in(own_key, 6), axis_at), (parts,), jnp.float32, smallest / len(cuts), largest / len(cuts))
        gain = gain * jnp.repeat(jnp.exp(draws), shape[axis_at] // parts).reshape((-1,) + (1,) * (len(shape) - 1 - axis_at))
    return gain


def noise(own_key, shape, width, reach, cuts=(), held_as=jnp.bfloat16):
    entries = width * jax.random.normal(own_key, shape, jnp.float32)
    if cuts:
        entries = entries * block_levels(own_key, shape, cuts, -0.22, 0.18)
    return jnp.clip(entries, -reach, reach).astype(held_as)


def setup_inputs(seed: int = 0) -> dict:
    seeds = jax.random.split(jax.random.key(seed), 9)
    fine_rows = noise(seeds[0], (DOCS, DOC_LEN, DF), 1.0, 6.0, ((0, 4), (1, 8)))
    segment_ids = draw_segment_ids(jax.random.fold_in(seeds[8], 71), 0)
    pool_gain = jnp.clip(1.0 + 0.18 * jax.random.normal(seeds[2], (DF,), jnp.float32), 0.1, 1.9)
    w_in = noise(seeds[3], (DF, D), DF ** -0.5, 0.125, ((0, 4), (1, 8)))
    w_gate = noise(seeds[4], (D, FF), D ** -0.5, 0.0625, ((0, 4), (1, 8)))
    w_up = noise(seeds[5], (D, FF), D ** -0.5, 0.0625, ((0, 4), (1, 8)))
    w_down = noise(seeds[6], (FF, D), FF ** -0.5, 0.046875, ((0, 8), (1, 4)))
    out_grad = noise(seeds[7], (DOCS, ROWS, D), 1.0, 6.0, ((0, 4),))
    return dict(fine_rows=fine_rows, segment_ids=segment_ids, pool_gain=pool_gain, w_in=w_in, w_gate=w_gate, w_up=w_up, w_down=w_down, out_grad=out_grad)


norm_eps = 1e-06

def silu_parts(gate_value):
    sigma = jax.nn.sigmoid(gate_value)
    return (gate_value * sigma, sigma * (1.0 + gate_value * (1.0 - sigma)))

def rounded_total(terms):
    rounded = lax.optimization_barrier(terms.astype(jnp.bfloat16))
    return lax.optimization_barrier(jnp.sum(rounded.astype(jnp.float32), axis=1))

def reference(fine_rows, segment_ids, pool_gain, w_in, w_gate, w_up, w_down, out_grad):
    block = FF // N_SEQ
    down_blocks = w_down.reshape(N_SEQ, block, D).astype(jnp.float32)
    gate_blocks = w_gate.reshape(D, N_SEQ, block).astype(jnp.float32)
    up_blocks = w_up.reshape(D, N_SEQ, block).astype(jnp.float32)
    slots = jnp.arange(SEG_CAP, dtype=jnp.int32)

    def one_document(inputs):
        rows_doc, index_doc, grad_doc = inputs
        shard_rows = rows_doc.reshape(N_SEQ, TOK_DEV, DF).astype(jnp.float32)
        shard_index = index_doc.reshape(N_SEQ, TOK_DEV)
        member = (shard_index[:, None, :] == slots[None, :, None]).astype(jnp.float32)
        segment_sums = jnp.einsum('sct,std->scd', member, shard_rows).reshape(ROWS, DF)
        inv_rms = lax.rsqrt(lax.optimization_barrier(jnp.mean(segment_sums * segment_sums, axis=1, keepdims=True)) + norm_eps)
        pooled = (segment_sums * inv_rms * pool_gain).astype(jnp.bfloat16)
        coarse_x = jnp.dot(pooled, w_in, preferred_element_type=jnp.float32).astype(jnp.bfloat16)
        gate_value = jnp.dot(coarse_x, w_gate, preferred_element_type=jnp.float32)
        up_value = jnp.dot(coarse_x, w_up, preferred_element_type=jnp.float32)
        activated, derivative = silu_parts(gate_value)
        hidden = (activated * up_value).astype(jnp.bfloat16)
        hidden_blocks = hidden.reshape(ROWS, N_SEQ, block).astype(jnp.float32)
        down_sum = rounded_total(jnp.einsum('rsf,sfd->rsd', hidden_blocks, down_blocks))
        coarse_out = (coarse_x.astype(jnp.float32) + down_sum).astype(jnp.bfloat16)
        grad_hidden = jnp.dot(grad_doc, w_down.T, preferred_element_type=jnp.float32)
        grad_gate = (grad_hidden * up_value * derivative).astype(jnp.bfloat16)
        grad_up = (grad_hidden * activated).astype(jnp.bfloat16)
        gate_terms = jnp.einsum('rsf,dsf->rsd', grad_gate.reshape(ROWS, N_SEQ, block).astype(jnp.float32), gate_blocks)
        up_terms = jnp.einsum('rsf,dsf->rsd', grad_up.reshape(ROWS, N_SEQ, block).astype(jnp.float32), up_blocks)
        back_sum = rounded_total(gate_terms + up_terms)
        grad_x = (grad_doc.astype(jnp.float32) + back_sum).astype(jnp.bfloat16)
        grad_pooled = jnp.dot(grad_x, w_in.T, preferred_element_type=jnp.float32)
        weighted = grad_pooled * pool_gain
        inner = lax.optimization_barrier(jnp.mean(weighted * segment_sums, axis=1, keepdims=True))
        grad_sums = inv_rms * weighted - segment_sums * (inv_rms * inv_rms * inv_rms) * inner
        grad_shards = grad_sums.reshape(N_SEQ, SEG_CAP, DF)
        fine_doc = jnp.einsum('sct,scd->std', member, grad_shards, precision=lax.Precision.HIGHEST)
        return (coarse_out, fine_doc.reshape(DOC_LEN, DF).astype(jnp.bfloat16))
    coarse_out, fine_grad = lax.map(one_document, (fine_rows, segment_ids, out_grad))
    return (coarse_out, fine_grad)
```

```python
import jax
import jax.numpy as jnp
from jax import lax
from jax.sharding import PartitionSpec as P

SEG_CAP = 8


norm_eps = 1e-06
bf16 = jnp.bfloat16
f32 = jnp.float32


def silu_parts(gate_value):
    sigma = jax.nn.sigmoid(gate_value)
    return (gate_value * sigma, sigma * (1.0 + gate_value * (1.0 - sigma)))


def matmul(a, b):
    return jnp.dot(a, b, preferred_element_type=f32)


def matmul_t(a, b):
    return lax.dot_general(a, b, (((1,), (1,)), ((), ())), preferred_element_type=f32)


def swap_pairs(grps, seqs):
    halves = seqs // grps
    return [
        (g * seqs + p * halves + h, p * seqs + g * halves + h)
        for g in range(grps)
        for p in range(grps)
        for h in range(halves)
    ]


def grp_total(partial_value):
    return lax.psum_scatter(
        partial_value.astype(bf16), "grp", scatter_dimension=0, tiled=True
    ).astype(f32)


def make_shards(grps, seqs):
    halves = seqs // grps
    pairs = swap_pairs(grps, seqs)

    def swap(value):
        return lax.ppermute(value, ("grp", "seq"), pairs)

    def shards(fine_rows, segment_ids, pool_gain, w_in, w_gate, w_up, w_down, out_grad):
        rows_here = fine_rows[0]
        index_here = segment_ids[0]
        feat, width = w_in.shape
        slots = jnp.arange(SEG_CAP, dtype=jnp.int32)
        member = index_here[None, :] == slots[:, None]
        segment_sums = matmul(member.astype(bf16), rows_here)
        inv_rms = lax.rsqrt(jnp.mean(segment_sums * segment_sums, axis=1, keepdims=True) + norm_eps)
        pooled = (segment_sums * inv_rms * pool_gain).astype(bf16)
        live_count = jnp.max(index_here) + 1
        packed = jnp.concatenate(
            [pooled, jnp.full((1, pooled.shape[1]), live_count.astype(bf16))], axis=0
        )
        gathered = lax.all_gather(packed, "seq", axis=0)
        shard_counts = gathered[:, SEG_CAP, 0].astype(jnp.int32)
        gathered = gathered[:, :SEG_CAP].reshape(seqs * SEG_CAP, -1)
        offsets = jnp.cumsum(shard_counts) - shard_counts
        slot_count = seqs * SEG_CAP
        within = jnp.tile(slots, seqs)
        target = jnp.repeat(offsets, SEG_CAP) + within
        is_live = within < jnp.repeat(shard_counts, SEG_CAP)
        rows = slot_count * 3 // 4
        select = (target[None, :] == jnp.arange(rows, dtype=jnp.int32)[:, None]) & is_live[None, :]
        selector = select.astype(bf16)
        work_in = matmul(selector, gathered).astype(bf16)
        work_in = lax.all_to_all(
            work_in.reshape(rows, grps, feat), "grp", split_axis=1, concat_axis=0
        ).reshape(grps * rows, feat)
        x_cols = grp_total(matmul(work_in, w_in)).astype(bf16)

        seq_at = lax.axis_index("seq")
        block = w_gate.shape[0]
        piece = block // seqs
        grad_here = out_grad[0].reshape(slot_count, grps, seqs, piece)
        grad_part = lax.dynamic_index_in_dim(grad_here, seq_at, 2, keepdims=False)
        grad_part = matmul(selector, grad_part.reshape(slot_count, grps * piece)).astype(bf16)
        grad_part = lax.all_to_all(
            grad_part.reshape(rows, grps, piece), "grp", split_axis=1, concat_axis=0
        ).reshape(grps * rows, piece)
        work_grad = lax.all_gather(grad_part, "seq", axis=1, tiled=True)
        grad_hidden = grp_total(matmul_t(work_grad, w_down))

        def spread(cols):
            every = lax.all_gather(swap(cols), "seq", axis=0)
            every = every.reshape(grps, halves, rows, width)
            return every.transpose(0, 2, 1, 3).reshape(grps * rows, halves * width)

        def column_total(part):
            part = part.astype(bf16).reshape(grps, rows, halves, width)
            part = part.transpose(0, 2, 1, 3).reshape(seqs * rows, width)
            return swap(lax.psum_scatter(part, "seq", scatter_dimension=0, tiled=True)).astype(f32)

        coarse_x = spread(x_cols)
        gate_value = grp_total(matmul(coarse_x, w_gate))
        up_value = grp_total(matmul(coarse_x, w_up))
        activated, derivative = silu_parts(gate_value)
        hidden = (activated * up_value).astype(bf16)
        grad_gate = (grad_hidden * up_value * derivative).astype(bf16)
        grad_up = (grad_hidden * activated).astype(bf16)
        grad_gate = lax.all_gather(grad_gate, "grp", axis=0, tiled=True)
        grad_up = lax.all_gather(grad_up, "grp", axis=0, tiled=True)
        hidden = lax.all_gather(hidden, "grp", axis=0, tiled=True)
        back_cols = column_total(matmul_t(grad_gate, w_gate) + matmul_t(grad_up, w_up))
        down_cols = column_total(matmul(hidden, w_down))
        out_cols = (x_cols.astype(f32) + down_cols).astype(bf16)
        out_cols = matmul(selector.T, out_cols).astype(bf16)

        grad_cols = lax.dynamic_slice_in_dim(out_grad[0], seq_at * width, width, 1)
        grad_cols = matmul(selector, grad_cols)
        grad_x = (back_cols + grad_cols).astype(bf16)
        grad_x = lax.all_gather(grad_x, "grp", axis=0, tiled=True)
        term = matmul_t(grad_x, w_in).astype(bf16)
        term = lax.all_to_all(
            term.reshape(grps, rows, feat), "grp", split_axis=0, concat_axis=1
        ).reshape(rows, grps * feat)
        term = matmul(selector.T, term).astype(bf16)
        grad_pooled = lax.psum_scatter(term, "seq", scatter_dimension=0, tiled=True).astype(f32)
        weighted = grad_pooled * pool_gain
        inner = jnp.mean(weighted * segment_sums, axis=1, keepdims=True)
        grad_sums = inv_rms * weighted - segment_sums * (inv_rms * inv_rms * inv_rms) * inner
        fine_grad = matmul(member.astype(bf16).T, grad_sums.astype(bf16)).astype(bf16)
        return (out_cols[None], fine_grad[None])

    return shards


def solution(mesh):
    return jax.shard_map(
        make_shards(mesh.shape["grp"], mesh.shape["seq"]),
        mesh=mesh,
        in_specs=(
            P("grp", "seq", None),
            P("grp", "seq"),
            P(),
            P("grp", "seq"),
            P("grp", "seq"),
            P("grp", "seq"),
            P("seq", "grp"),
            P("grp", None, None),
        ),
        out_specs=(P("grp", None, "seq"), P("grp", "seq", None)),
        check_vma=False,
    )
```

```python
import functools

import jax
import jax.numpy as jnp
from jax import lax
from jax.experimental import pallas as pl
from jax.experimental.pallas import tpu as pltpu
from jax.sharding import PartitionSpec as P

SEG_CAP = 8


norm_eps = 1e-06
bf16 = jnp.bfloat16
f32 = jnp.float32


def silu_parts(gate_value):
    sigma = jax.nn.sigmoid(gate_value)
    return (gate_value * sigma, sigma * (1.0 + gate_value * (1.0 - sigma)))


def matmul(a, b):
    return jnp.dot(a, b, preferred_element_type=f32)


def matmul_t(a, b):
    return lax.dot_general(a, b, (((1,), (1,)), ((), ())), preferred_element_type=f32)


def greet(axis, count):
    me = lax.axis_index(axis)
    barrier = pltpu.get_barrier_semaphore()
    for step in range(1, count):
        pl.semaphore_signal(
            barrier,
            inc=1,
            device_id={axis: lax.rem(me + step, count)},
            device_id_type=pl.DeviceIdType.MESH,
        )
    pl.semaphore_wait(barrier, count - 1)
    return me


def exchange_kernel(axis, count, modes, *refs):
    arrays = len(modes)
    ins, outs = refs[:arrays], refs[arrays : 2 * arrays]
    send_sem, recv_sem, own_sem = refs[2 * arrays :]
    me = greet(axis, count)
    copies = []
    for at, mode in enumerate(modes):
        for step in range(1, count):
            peer = lax.rem(me + step, count)
            copy = pltpu.make_async_remote_copy(
                src_ref=ins[at].at[peer] if mode == "swap" else ins[at],
                dst_ref=outs[at].at[me],
                send_sem=send_sem.at[at, step],
                recv_sem=recv_sem.at[at, step],
                device_id={axis: peer},
                device_id_type=pl.DeviceIdType.MESH,
            )
            copy.start()
            copies.append(copy)
        copy = pltpu.make_async_copy(
            ins[at].at[me] if mode == "swap" else ins[at], outs[at].at[me], own_sem.at[at]
        )
        copy.start()
        copies.append(copy)
    for copy in copies:
        copy.wait()


def exchange(arrays, axis, count, modes, ident):
    shapes = [a.shape if m == "swap" else (count,) + a.shape for a, m in zip(arrays, modes)]
    return pl.pallas_call(
        functools.partial(exchange_kernel, axis, count, modes),
        out_shape=[jax.ShapeDtypeStruct(sh, a.dtype) for sh, a in zip(shapes, arrays)],
        in_specs=[pl.BlockSpec(memory_space=pltpu.VMEM)] * len(arrays),
        out_specs=[pl.BlockSpec(memory_space=pltpu.VMEM)] * len(arrays),
        scratch_shapes=[
            pltpu.SemaphoreType.DMA((len(arrays), count)),
            pltpu.SemaphoreType.DMA((len(arrays), count)),
            pltpu.SemaphoreType.DMA((len(arrays),)),
        ],
        compiler_params=pltpu.CompilerParams(collective_id=ident, has_side_effects=True),
        name="exchange_%d" % ident,
    )(*arrays)


def block_kernel(
    grps, rows, tile, width, x_ref, gh_ref, gate_hbm, up_hbm, down_hbm, back_out, down_out,
    gate_w, up_w, down_w, part, part_in, held, back_acc, down_acc,
    load_sem, send_a, recv_a, send_b, recv_b,
):
    block, hidden_width = gate_w.shape
    tiles = hidden_width // tile
    col = back_acc.shape[2]
    cols = block // col
    loads = [
        pltpu.make_async_copy(src, dst, load_sem.at[at])
        for at, (src, dst) in enumerate(((gate_hbm, gate_w), (up_hbm, up_w), (down_hbm, down_w)))
    ]
    for load in loads:
        load.start()
    me = greet("grp", grps)

    def part_copy(t, step):
        peer = lax.rem(me + step, grps)
        return pltpu.make_async_remote_copy(
            src_ref=part.at[t, peer],
            dst_ref=part_in.at[t, step - 1],
            send_sem=send_a.at[t, step],
            recv_sem=recv_a.at[t, step],
            device_id={"grp": peer},
            device_id_type=pl.DeviceIdType.MESH,
        )

    def held_copy(t, step):
        return pltpu.make_async_remote_copy(
            src_ref=held.at[t, me],
            dst_ref=held.at[t, me],
            send_sem=send_b.at[t, step],
            recv_sem=recv_b.at[t, step],
            device_id={"grp": lax.rem(me + step, grps)},
            device_id_type=pl.DeviceIdType.MESH,
        )

    loads[0].wait()
    loads[1].wait()

    @pl.loop(0, tiles)
    def _(t):
        here = pl.ds(pl.multiple_of(t * tile, tile), tile)
        for at, weight in enumerate((gate_w, up_w)):
            value = matmul(x_ref[...], weight[:, here]).astype(bf16)
            part[t, :, at] = value.reshape(grps, rows, tile)
        for step in range(1, grps):
            part_copy(t, step).start()

    @pl.loop(0, tiles)
    def _(t):
        gate_value = part[t, me, 0].astype(f32)
        up_value = part[t, me, 1].astype(f32)
        for step in range(1, grps):
            part_copy(t, step).wait_recv()
            gate_value = gate_value + part_in[t, step - 1, 0].astype(f32)
            up_value = up_value + part_in[t, step - 1, 1].astype(f32)
        grad_hidden = gh_ref[:, pl.ds(pl.multiple_of(t * tile, tile), tile)]
        activated, derivative = silu_parts(gate_value)
        held[t, me, 0] = (grad_hidden * up_value * derivative).astype(bf16)
        held[t, me, 1] = (grad_hidden * activated).astype(bf16)
        held[t, me, 2] = (activated * up_value).astype(bf16)
        for step in range(1, grps):
            held_copy(t, step).start()

    loads[2].wait()

    @pl.loop(0, tiles)
    def _(t):
        here = pl.ds(pl.multiple_of(t * tile, tile), tile)
        for step in range(1, grps):
            held_copy(t, step).wait_recv()
        grad_gate = held[t, :, 0].reshape(grps * rows, tile)
        grad_up = held[t, :, 1].reshape(grps * rows, tile)
        hidden = held[t, :, 2].reshape(grps * rows, tile)

        @pl.loop(0, cols)
        def _(c):
            there = pl.ds(pl.multiple_of(c * col, col), col)
            back = matmul_t(grad_gate, gate_w[there, here]) + matmul_t(grad_up, up_w[there, here])
            down = matmul(hidden, down_w[here, there])

            @pl.when(t == 0)
            def _():
                back_acc[c] = back
                down_acc[c] = down

            @pl.when(t > 0)
            def _():
                back_acc[c] += back
                down_acc[c] += down

    halves = block // width
    fits = width // col
    for c in range(cols):
        half, at = c // fits, c % fits
        for acc, out in ((back_acc, back_out), (down_acc, down_out)):
            value = acc[c].astype(bf16)
            for g in range(grps):
                out[g * halves + half, :, at * col : (at + 1) * col] = value[
                    g * rows : (g + 1) * rows
                ]

    @pl.loop(0, tiles)
    def _(t):
        for step in range(1, grps):
            part_copy(t, step).wait_send()
            held_copy(t, step).wait_send()


def coarse_block(coarse_x, grad_hidden, w_gate, w_up, w_down, grps, rows, width, ident):
    block, hidden_width = w_gate.shape
    tile = min(512, hidden_width)
    tiles = hidden_width // tile
    col = min(512, width)
    seqs = grps * (block // width)
    vmem = pl.BlockSpec(memory_space=pltpu.VMEM)
    hbm = pl.BlockSpec(memory_space=pl.ANY)
    return pl.pallas_call(
        functools.partial(block_kernel, grps, rows, tile, width),
        out_shape=[jax.ShapeDtypeStruct((seqs, rows, width), bf16)] * 2,
        in_specs=[vmem, vmem, hbm, hbm, hbm],
        out_specs=[vmem, vmem],
        scratch_shapes=[
            pltpu.VMEM(w_gate.shape, bf16),
            pltpu.VMEM(w_up.shape, bf16),
            pltpu.VMEM(w_down.shape, bf16),
            pltpu.VMEM((tiles, grps, 2, rows, tile), bf16),
            pltpu.VMEM((tiles, grps - 1, 2, rows, tile), bf16),
            pltpu.VMEM((tiles, grps, 3, rows, tile), bf16),
            pltpu.VMEM((block // col, grps * rows, col), f32),
            pltpu.VMEM((block // col, grps * rows, col), f32),
            pltpu.SemaphoreType.DMA((3,)),
        ]
        + [pltpu.SemaphoreType.DMA((tiles, grps))] * 4,
        compiler_params=pltpu.CompilerParams(
            collective_id=ident, has_side_effects=True, vmem_limit_bytes=56 * 2**20
        ),
        name="coarse_block",
    )(coarse_x, grad_hidden, w_gate, w_up, w_down)


def swap_pairs(grps, seqs):
    halves = seqs // grps
    return [
        (g * seqs + p * halves + h, p * seqs + g * halves + h)
        for g in range(grps)
        for p in range(grps)
        for h in range(halves)
    ]


def grp_total(partial_value):
    return lax.psum_scatter(
        partial_value.astype(bf16), "grp", scatter_dimension=0, tiled=True
    ).astype(f32)


def make_shards(grps, seqs):
    halves = seqs // grps
    pairs = swap_pairs(grps, seqs)

    def swap(value):
        return lax.ppermute(value, ("grp", "seq"), pairs)

    def shards(fine_rows, segment_ids, pool_gain, w_in, w_gate, w_up, w_down, out_grad):
        rows_here = fine_rows[0]
        index_here = segment_ids[0]
        feat, width = w_in.shape
        slots = jnp.arange(SEG_CAP, dtype=jnp.int32)
        member = index_here[None, :] == slots[:, None]
        segment_sums = matmul(member.astype(bf16), rows_here)
        inv_rms = lax.rsqrt(jnp.mean(segment_sums * segment_sums, axis=1, keepdims=True) + norm_eps)
        pooled = (segment_sums * inv_rms * pool_gain).astype(bf16)
        live_count = jnp.max(index_here) + 1
        packed = jnp.concatenate(
            [pooled, jnp.full(pooled.shape, live_count.astype(bf16))], axis=0
        )
        gathered = exchange([packed], "seq", seqs, ("share",), 0)[0]
        shard_counts = gathered[:, SEG_CAP, 0].astype(jnp.int32)
        gathered = gathered[:, :SEG_CAP].reshape(seqs * SEG_CAP, -1)
        offsets = jnp.cumsum(shard_counts) - shard_counts
        slot_count = seqs * SEG_CAP
        within = jnp.tile(slots, seqs)
        target = jnp.repeat(offsets, SEG_CAP) + within
        is_live = within < jnp.repeat(shard_counts, SEG_CAP)
        rows = slot_count * 3 // 4
        select = (target[None, :] == jnp.arange(rows, dtype=jnp.int32)[:, None]) & is_live[None, :]
        selector = select.astype(bf16)
        work_in = matmul(selector, gathered).astype(bf16)
        seq_at = lax.axis_index("seq")
        block = w_gate.shape[0]
        piece = block // seqs
        grad_here = out_grad[0].reshape(slot_count, grps, seqs, piece)
        grad_part = lax.dynamic_index_in_dim(grad_here, seq_at, 2, keepdims=False)
        grad_part = matmul(selector, grad_part.reshape(slot_count, grps * piece)).astype(bf16)
        work_in, grad_part = exchange(
            [
                work_in.reshape(rows, grps, feat).transpose(1, 0, 2),
                grad_part.reshape(rows, grps, piece).transpose(1, 0, 2),
            ],
            "grp",
            grps,
            ("swap", "swap"),
            1,
        )
        x_part = matmul(work_in.reshape(grps * rows, feat), w_in).astype(bf16)
        x_part = exchange([x_part.reshape(grps, rows, width)], "grp", grps, ("swap",), 2)[0]
        x_cols = jnp.sum(x_part.astype(f32), axis=0).astype(bf16)
        work_grad = exchange(
            [grad_part.reshape(grps * rows, piece)], "seq", seqs, ("share",), 3
        )[0]
        work_grad = work_grad.transpose(1, 0, 2).reshape(grps * rows, block)
        grad_hidden = grp_total(matmul_t(work_grad, w_down))

        def spread(cols):
            every = exchange([swap(cols)], "seq", seqs, ("share",), 4)[0]
            every = every.reshape(grps, halves, rows, width)
            return every.transpose(0, 2, 1, 3).reshape(grps * rows, halves * width)

        coarse_x = spread(x_cols)
        back_part, down_part = coarse_block(
            coarse_x, grad_hidden, w_gate, w_up, w_down, grps, rows, width, 5
        )
        back_in, down_in = exchange([back_part, down_part], "seq", seqs, ("swap", "swap"), 6)
        back_cols = swap(jnp.sum(back_in.astype(f32), axis=0).astype(bf16)).astype(f32)
        down_cols = swap(jnp.sum(down_in.astype(f32), axis=0).astype(bf16)).astype(f32)
        out_cols = (x_cols.astype(f32) + down_cols).astype(bf16)
        out_cols = matmul(selector.T, out_cols).astype(bf16)

        grad_cols = lax.dynamic_slice_in_dim(out_grad[0], seq_at * width, width, 1)
        grad_cols = matmul(selector, grad_cols)
        grad_x = (back_cols + grad_cols).astype(bf16)
        grad_x = exchange([grad_x], "grp", grps, ("share",), 7)[0].reshape(grps * rows, width)
        term = matmul_t(grad_x, w_in).astype(bf16)
        term = exchange([term.reshape(grps, rows, feat)], "grp", grps, ("swap",), 8)[0]
        term = term.transpose(1, 0, 2).reshape(rows, grps * feat)
        term = matmul(selector.T, term).astype(bf16).reshape(seqs, SEG_CAP, grps * feat)
        term = exchange([term], "seq", seqs, ("swap",), 9)[0]
        grad_pooled = jnp.sum(term.astype(f32), axis=0)
        weighted = grad_pooled * pool_gain
        inner = jnp.mean(weighted * segment_sums, axis=1, keepdims=True)
        grad_sums = inv_rms * weighted - segment_sums * (inv_rms * inv_rms * inv_rms) * inner
        fine_grad = matmul(member.astype(bf16).T, grad_sums.astype(bf16)).astype(bf16)
        return (out_cols[None], fine_grad[None])

    return shards


def solution(mesh):
    return jax.shard_map(
        make_shards(mesh.shape["grp"], mesh.shape["seq"]),
        mesh=mesh,
        in_specs=(
            P("grp", "seq", None),
            P("grp", "seq"),
            P(),
            P("grp", "seq"),
            P("grp", "seq"),
            P("grp", "seq"),
            P("seq", "grp"),
            P("grp", None, None),
        ),
        out_specs=(P("grp", None, "seq"), P("grp", "seq", None)),
        check_vma=False,
    )
```

```python
import functools

import jax
import jax.numpy as jnp
from jax import lax
from jax.experimental import pallas as pl
from jax.experimental.pallas import tpu as pltpu
from jax.sharding import PartitionSpec as P

SEG_CAP = 8


norm_eps = 1e-06
bf16 = jnp.bfloat16
f32 = jnp.float32


def silu_parts(gate_value):
    sigma = jax.nn.sigmoid(gate_value)
    return (gate_value * sigma, sigma * (1.0 + gate_value * (1.0 - sigma)))


def matmul(a, b):
    return jnp.dot(a, b, preferred_element_type=f32)


def matmul_t(a, b):
    return lax.dot_general(a, b, (((1,), (1,)), ((), ())), preferred_element_type=f32)


def greet(axis, count):
    me = lax.axis_index(axis)
    barrier = pltpu.get_barrier_semaphore()
    for step in range(1, count):
        pl.semaphore_signal(
            barrier,
            inc=1,
            device_id={axis: lax.rem(me + step, count)},
            device_id_type=pl.DeviceIdType.MESH,
        )
    pl.semaphore_wait(barrier, count - 1)
    return me


def exchange_kernel(axis, count, modes, *refs):
    arrays = len(modes)
    ins, outs = refs[:arrays], refs[arrays : 2 * arrays]
    send_sem, recv_sem, own_sem = refs[2 * arrays :]
    me = greet(axis, count)
    copies = []
    for at, mode in enumerate(modes):
        for step in range(1, count):
            peer = lax.rem(me + step, count)
            copy = pltpu.make_async_remote_copy(
                src_ref=ins[at].at[peer] if mode == "swap" else ins[at],
                dst_ref=outs[at].at[me],
                send_sem=send_sem.at[at, step],
                recv_sem=recv_sem.at[at, step],
                device_id={axis: peer},
                device_id_type=pl.DeviceIdType.MESH,
            )
            copy.start()
            copies.append(copy)
        copy = pltpu.make_async_copy(
            ins[at].at[me] if mode == "swap" else ins[at], outs[at].at[me], own_sem.at[at]
        )
        copy.start()
        copies.append(copy)
    for copy in copies:
        copy.wait()


def exchange(arrays, axis, count, modes, ident):
    shapes = [a.shape if m == "swap" else (count,) + a.shape for a, m in zip(arrays, modes)]
    return pl.pallas_call(
        functools.partial(exchange_kernel, axis, count, modes),
        out_shape=[jax.ShapeDtypeStruct(sh, a.dtype) for sh, a in zip(shapes, arrays)],
        in_specs=[pl.BlockSpec(memory_space=pltpu.VMEM)] * len(arrays),
        out_specs=[pl.BlockSpec(memory_space=pltpu.VMEM)] * len(arrays),
        scratch_shapes=[
            pltpu.SemaphoreType.DMA((len(arrays), count)),
            pltpu.SemaphoreType.DMA((len(arrays), count)),
            pltpu.SemaphoreType.DMA((len(arrays),)),
        ],
        compiler_params=pltpu.CompilerParams(collective_id=ident, has_side_effects=True),
        name="exchange_%d" % ident,
    )(*arrays)


def block_kernel(
    grps, rows, tile, width, x_ref, gh_ref, gate_hbm, up_hbm, down_hbm, back_out, down_out,
    gate_w, up_w, down_w, part, part_in, held, back_acc, down_acc,
    load_sem, send_a, recv_a, send_b, recv_b,
):
    block, hidden_width = gate_w.shape
    tiles = hidden_width // tile
    col = back_acc.shape[2]
    cols = block // col
    loads = [
        pltpu.make_async_copy(src, dst, load_sem.at[at])
        for at, (src, dst) in enumerate(((gate_hbm, gate_w), (up_hbm, up_w), (down_hbm, down_w)))
    ]
    for load in loads:
        load.start()
    me = greet("grp", grps)

    def part_copy(t, step):
        peer = lax.rem(me + step, grps)
        return pltpu.make_async_remote_copy(
            src_ref=part.at[t, peer],
            dst_ref=part_in.at[t, step - 1],
            send_sem=send_a.at[t, step],
            recv_sem=recv_a.at[t, step],
            device_id={"grp": peer},
            device_id_type=pl.DeviceIdType.MESH,
        )

    def held_copy(t, step):
        return pltpu.make_async_remote_copy(
            src_ref=held.at[t, me],
            dst_ref=held.at[t, me],
            send_sem=send_b.at[t, step],
            recv_sem=recv_b.at[t, step],
            device_id={"grp": lax.rem(me + step, grps)},
            device_id_type=pl.DeviceIdType.MESH,
        )

    loads[0].wait()
    loads[1].wait()

    @pl.loop(0, tiles)
    def _(t):
        here = pl.ds(pl.multiple_of(t * tile, tile), tile)
        for at, weight in enumerate((gate_w, up_w)):
            value = matmul(x_ref[...], weight[:, here]).astype(bf16)
            part[t, :, at] = value.reshape(grps, rows, tile)
        for step in range(1, grps):
            part_copy(t, step).start()

    @pl.loop(0, tiles)
    def _(t):
        gate_value = part[t, me, 0].astype(f32)
        up_value = part[t, me, 1].astype(f32)
        for step in range(1, grps):
            part_copy(t, step).wait_recv()
            gate_value = gate_value + part_in[t, step - 1, 0].astype(f32)
            up_value = up_value + part_in[t, step - 1, 1].astype(f32)
        grad_hidden = gh_ref[:, pl.ds(pl.multiple_of(t * tile, tile), tile)]
        activated, derivative = silu_parts(gate_value)
        held[t, me, 0] = (grad_hidden * up_value * derivative).astype(bf16)
        held[t, me, 1] = (grad_hidden * activated).astype(bf16)
        held[t, me, 2] = (activated * up_value).astype(bf16)
        for step in range(1, grps):
            held_copy(t, step).start()

    loads[2].wait()

    @pl.loop(0, tiles)
    def _(t):
        here = pl.ds(pl.multiple_of(t * tile, tile), tile)
        for step in range(1, grps):
            held_copy(t, step).wait_recv()
        grad_gate = held[t, :, 0].reshape(grps * rows, tile)
        grad_up = held[t, :, 1].reshape(grps * rows, tile)
        hidden = held[t, :, 2].reshape(grps * rows, tile)

        @pl.loop(0, cols)
        def _(c):
            there = pl.ds(pl.multiple_of(c * col, col), col)
            back = matmul_t(grad_gate, gate_w[there, here]) + matmul_t(grad_up, up_w[there, here])
            down = matmul(hidden, down_w[here, there])

            @pl.when(t == 0)
            def _():
                back_acc[c] = back
                down_acc[c] = down

            @pl.when(t > 0)
            def _():
                back_acc[c] += back
                down_acc[c] += down

    halves = block // width
    fits = width // col
    for c in range(cols):
        half, at = c // fits, c % fits
        for acc, out in ((back_acc, back_out), (down_acc, down_out)):
            value = acc[c].astype(bf16)
            for g in range(grps):
                out[g * halves + half, :, at * col : (at + 1) * col] = value[
                    g * rows : (g + 1) * rows
                ]

    @pl.loop(0, tiles)
    def _(t):
        for step in range(1, grps):
            part_copy(t, step).wait_send()
            held_copy(t, step).wait_send()


def coarse_block(coarse_x, grad_hidden, w_gate, w_up, w_down, grps, rows, width, ident):
    block, hidden_width = w_gate.shape
    tile = min(512, hidden_width)
    tiles = hidden_width // tile
    col = min(512, width)
    seqs = grps * (block // width)
    vmem = pl.BlockSpec(memory_space=pltpu.VMEM)
    hbm = pl.BlockSpec(memory_space=pl.ANY)
    return pl.pallas_call(
        functools.partial(block_kernel, grps, rows, tile, width),
        out_shape=[jax.ShapeDtypeStruct((seqs, rows, width), bf16)] * 2,
        in_specs=[vmem, vmem, hbm, hbm, hbm],
        out_specs=[vmem, vmem],
        scratch_shapes=[
            pltpu.VMEM(w_gate.shape, bf16),
            pltpu.VMEM(w_up.shape, bf16),
            pltpu.VMEM(w_down.shape, bf16),
            pltpu.VMEM((tiles, grps, 2, rows, tile), bf16),
            pltpu.VMEM((tiles, grps - 1, 2, rows, tile), bf16),
            pltpu.VMEM((tiles, grps, 3, rows, tile), bf16),
            pltpu.VMEM((block // col, grps * rows, col), f32),
            pltpu.VMEM((block // col, grps * rows, col), f32),
            pltpu.SemaphoreType.DMA((3,)),
        ]
        + [pltpu.SemaphoreType.DMA((tiles, grps))] * 4,
        compiler_params=pltpu.CompilerParams(
            collective_id=ident, has_side_effects=True, vmem_limit_bytes=56 * 2**20
        ),
        name="coarse_block",
    )(coarse_x, grad_hidden, w_gate, w_up, w_down)


def swap_pairs(grps, seqs):
    halves = seqs // grps
    return [
        (g * seqs + p * halves + h, p * seqs + g * halves + h)
        for g in range(grps)
        for p in range(grps)
        for h in range(halves)
    ]


def grp_total(partial_value):
    return lax.psum_scatter(
        partial_value.astype(bf16), "grp", scatter_dimension=0, tiled=True
    ).astype(f32)


def make_shards(grps, seqs):
    halves = seqs // grps
    pairs = swap_pairs(grps, seqs)

    def swap(value):
        return lax.ppermute(value, ("grp", "seq"), pairs)

    def shards(fine_rows, segment_ids, pool_gain, w_in, w_gate, w_up, w_down, out_grad):
        rows_here = fine_rows[0]
        index_here = segment_ids[0]
        feat, width = w_in.shape
        full_in = lax.all_gather(w_in, "grp", axis=0, tiled=True)
        slots = jnp.arange(SEG_CAP, dtype=jnp.int32)
        member = index_here[None, :] == slots[:, None]
        segment_sums = matmul(member.astype(bf16), rows_here)
        inv_rms = lax.rsqrt(jnp.mean(segment_sums * segment_sums, axis=1, keepdims=True) + norm_eps)
        pooled = (segment_sums * inv_rms * pool_gain).astype(bf16)
        live_count = jnp.max(index_here) + 1
        packed = jnp.concatenate(
            [pooled, jnp.full((SEG_CAP, 128), live_count.astype(bf16))], axis=1
        )
        gathered = exchange([packed], "seq", seqs, ("share",), 0)[0]
        shard_counts = gathered[:, 0, -1].astype(jnp.int32)
        gathered = gathered[:, :, :-128].reshape(seqs * SEG_CAP, -1)
        offsets = jnp.cumsum(shard_counts) - shard_counts
        slot_count = seqs * SEG_CAP
        within = jnp.tile(slots, seqs)
        target = jnp.repeat(offsets, SEG_CAP) + within
        is_live = within < jnp.repeat(shard_counts, SEG_CAP)
        rows = slot_count * 3 // 4
        select = (target[None, :] == jnp.arange(rows, dtype=jnp.int32)[:, None]) & is_live[None, :]
        selector = select.astype(bf16)
        work_in = matmul(selector, gathered).astype(bf16)
        seq_at = lax.axis_index("seq")
        block = w_gate.shape[0]
        piece = block // seqs
        grad_here = out_grad[0].reshape(slot_count, grps, seqs, piece)
        grad_part = lax.dynamic_index_in_dim(grad_here, seq_at, 2, keepdims=False)
        grad_part = matmul(selector, grad_part.reshape(slot_count, grps * piece)).astype(bf16)
        grad_part = exchange(
            [grad_part.reshape(rows, grps, piece).transpose(1, 0, 2)], "grp", grps, ("swap",), 1
        )[0]
        work_grad = exchange(
            [grad_part.reshape(grps * rows, piece)], "seq", seqs, ("share",), 3
        )[0]
        work_grad = work_grad.transpose(1, 0, 2).reshape(grps * rows, block)
        work_in, work_grad = lax.optimization_barrier((work_in, work_grad))
        x_cols = matmul(work_in, full_in).astype(bf16)
        grad_hidden = grp_total(matmul_t(work_grad, w_down))

        def spread(cols):
            every = exchange([swap(cols)], "seq", seqs, ("share",), 4)[0]
            every = every.reshape(grps, halves, rows, width)
            return every.transpose(0, 2, 1, 3).reshape(grps * rows, halves * width)

        coarse_x = spread(x_cols)
        back_part, down_part = coarse_block(
            coarse_x, grad_hidden, w_gate, w_up, w_down, grps, rows, width, 5
        )
        back_in = exchange([back_part], "seq", seqs, ("swap",), 6)[0]
        back_cols = swap(jnp.sum(back_in.astype(f32), axis=0).astype(bf16)).astype(f32)
        down_in = lax.psum_scatter(
            down_part.reshape(seqs * rows, width), "seq", scatter_dimension=0, tiled=True
        )
        down_cols = swap(down_in).astype(f32)
        out_cols = (x_cols.astype(f32) + down_cols).astype(bf16)
        out_cols = matmul(selector.T, out_cols).astype(bf16)

        grad_cols = lax.dynamic_slice_in_dim(out_grad[0], seq_at * width, width, 1)
        grad_cols = matmul(selector, grad_cols)
        grad_x = (back_cols + grad_cols).astype(bf16)
        grad_x = matmul(selector.T, grad_x).astype(bf16)
        term = matmul_t(grad_x, full_in).astype(bf16).reshape(seqs, SEG_CAP, grps * feat)
        term = exchange([term], "seq", seqs, ("swap",), 9)[0]
        grad_pooled = jnp.sum(term.astype(f32), axis=0)
        weighted = grad_pooled * pool_gain
        inner = jnp.mean(weighted * segment_sums, axis=1, keepdims=True)
        grad_sums = inv_rms * weighted - segment_sums * (inv_rms * inv_rms * inv_rms) * inner
        fine_grad = matmul(member.astype(bf16).T, grad_sums.astype(bf16)).astype(bf16)
        return (out_cols[None], fine_grad[None])

    return shards


def solution(mesh):
    return jax.shard_map(
        make_shards(mesh.shape["grp"], mesh.shape["seq"]),
        mesh=mesh,
        in_specs=(
            P("grp", "seq", None),
            P("grp", "seq"),
            P(),
            P("grp", "seq"),
            P("grp", "seq"),
            P("grp", "seq"),
            P("seq", "grp"),
            P("grp", None, None),
        ),
        out_specs=(P("grp", None, "seq"), P("grp", "seq", None)),
        check_vma=False,
    )
```
